32 devices in a mesh: groups: 2 (over x), ctx: 16 (over z, y, core).
Axes of the slice: x: 2, y: 2, z: 4, core: 2. Of those that a mesh axis runs over, the one named last changes fastest.
Arguments:
- queries: bfloat16 [8, 128, 576], P('groups', 'ctx'), parts along dimension 0, may hold values from -300 to 300
- cache: bfloat16 [16384, 576], P(('groups', 'ctx')), parts along dimension 0, may hold values from -5 to 5
- page_row: int32 [128], P(('groups', 'ctx')), parts along dimension 0, may hold values from 0 to 3, as said below
- page_index: int32 [128], P(('groups', 'ctx')), parts along dimension 0, may hold values from 0 to 31, as said below
- lengths: int32 [8], P('groups'), parts along dimension 0, may hold values from 2 to 4096, as said below
- hidden_in: bfloat16 [8, 7168], P('groups', 'ctx'), parts along dimension 0, may hold values from -4 to 4
- norm_gain: float32 [7168], replicated, may hold values from 0.1 to 1.9
- absorb_value: bfloat16 [128, 512, 128], P('ctx'), may hold values from -0.5 to 0.5
- out_proj: bfloat16 [16384, 7168], P('ctx'), may hold values from -0.09375 to 0.09375
- gate_proj: bfloat16 [7168, 9216], P(None, 'ctx'), may hold values from -0.0625 to 0.0625
- up_proj: bfloat16 [7168, 9216], P(None, 'ctx'), may hold values from -0.0625 to 0.0625
- down_proj: bfloat16 [9216, 7168], P('ctx'), may hold values from -0.125 to 0.125
Outputs:
- mixed: bfloat16 [8, 7168], P('groups', 'ctx'), parts along dimension 0
The draws below stay inside these ranges and needn't reach their ends.
There are 2 independent parts, one for each index of `groups`. The reference program is written for one: setup_inputs(seed, part) draws one part's arguments, and reference() takes and returns one part's arrays. A program takes and returns all parts, laid end to end along the dimension named above; an argument that names none is the same for every part. Nothing has to cross between parts.
Inputs may be any that keep to these rules, and one draw needn't show every extreme that they name: `page_row`: every page belongs to a row; a row's pages are consecutive in page order and every row owns one or more. A row's pages have page_index 0, 1, 2 and so on in page order; slot j of a page holds the row's token page_index * 128 + j. `lengths`: every row's tokens fill its pages but for part of its last page, which holds two or more.
All inputs are finite; a program needn't handle non-finite values.
Results may differ from the reference program's by a relative error of at most 0.02.
Values may be sent and summed in bfloat16 or wider, within the bound.
No kernel may reach another device: no remote copies, remote signals or barrier semaphores. Data moves between devices by JAX's collectives and lax.ppermute only.
A program may use at most 128 MiB of HBM per device.

```python
import jax
import jax.numpy as jnp
from jax import lax

ROWS = 4
H = 128
LAT = 512
ROPE = 64
VHEAD = 128
D = 7168
FF = 9216
PAGE = 128
PAGES_DEV = 4
ENTRY = 576
PAGES = 64
CTX = 8192
N_CTX = 16


def page_layout(key):
    base_key = jax.random.fold_in(key, 101)
    key_a, key_b, key_c, key_d = jax.random.split(base_key, 4)
    most_weight = PAGES // ROWS
    first = jax.random.randint(key_a, (ROWS,), 0, most_weight + 1).astype(jnp.int32)
    second = jax.random.randint(key_b, (ROWS,), 0, most_weight + 1).astype(jnp.int32)
    row_order = jax.random.permutation(key_c, ROWS).astype(jnp.int32)
    row_rank = jnp.zeros((ROWS,), jnp.int32).at[row_order].set(jnp.arange(ROWS, dtype=jnp.int32))
    heavy = row_rank == 0
    row_weight = jnp.where(heavy, 0, 1 + first * second).astype(jnp.int32)
    heavy_pages = PAGES // 2
    spare = PAGES - heavy_pages - (ROWS - 1)
    base_pages = spare * row_weight // jnp.sum(row_weight)
    leftover = spare - jnp.sum(base_pages)
    extra = ((row_rank >= 1) & (row_rank <= leftover)).astype(jnp.int32)
    page_count = jnp.where(heavy, heavy_pages, 1 + base_pages + extra).astype(jnp.int32)
    ordered_counts = page_count[row_order]
    ordered_ends = jnp.cumsum(ordered_counts).astype(jnp.int32)
    page_ids = jnp.arange(PAGES, dtype=jnp.int32)
    place_in_order = jnp.sum((ordered_ends[None, :] <= page_ids[:, None]).astype(jnp.int32), axis=1)
    page_owner = row_order[place_in_order]
    ordered_starts = ordered_ends - ordered_counts
    row_start = jnp.zeros((ROWS,), jnp.int32).at[row_order].set(ordered_starts)
    page_place = page_ids - row_start[page_owner]
    tail_drawn = jax.random.randint(key_d, (ROWS,), 2, PAGE + 1).astype(jnp.int32)
    tail_fill = jnp.where(heavy, PAGE, tail_drawn).astype(jnp.int32)
    row_length = (page_count - 1) * PAGE + tail_fill
    return (page_owner, page_place, row_length, row_start)


def latent_cache(key):
    noise = jax.random.normal(jax.random.fold_in(key, 202), (CTX, ENTRY), jnp.float32)
    return jnp.clip(noise, -5.0, 5.0)


def draw_queries(key, part):
    query_key = jax.random.fold_in(key, 303)
    values = jax.random.normal(query_key, (ROWS, H, ENTRY), jnp.float32)
    page_owner, page_place, row_length, row_start = page_layout(key)
    anchors = latent_cache(key)[row_start * PAGE]
    unit = float(VHEAD + ROPE) ** 0.5 / float(ENTRY)
    values = values.at[:, 0, :].set(120.0 * unit * anchors)
    values = values.at[:, 1, :].set(240.0 * unit * anchors)
    values = values.at[:, 2, :].set(360.0 * unit * anchors)
    return jnp.clip(values, -300.0, 300.0).astype(jnp.bfloat16)


def draw_cache(key, part):
    return latent_cache(key).astype(jnp.bfloat16)


def draw_page_row(key, part):
    return page_layout(key)[0]


def draw_page_index(key, part):
    return page_layout(key)[1]


def draw_lengths(key, part):
    return page_layout(key)[2]


def level_of(rng, extent, cuts, smallest, high):
    factor_of, own = 1.0, jax.random.fold_in(rng, 6)
    for axis_at, blocks in cuts:
        draws = jnp.exp(jax.random.uniform(jax.random.fold_in(own, axis_at), (blocks,), jnp.float32, smallest / len(cuts), high / len(cuts)))
        factor_of = factor_of * jnp.repeat(draws, extent[axis_at] // blocks).reshape([-1 if axis == axis_at else 1 for axis in range(len(extent))])
    return factor_of


def normal_values(own_key, extent, spread, reach, cuts=(), held_as=jnp.bfloat16):
    level = level_of(own_key, extent, cuts, -0.22, 0.18) if cuts else 1.0
    entries = jax.random.normal(own_key, extent, jnp.float32) * spread * level
    return jnp.minimum(jnp.maximum(entries, -reach), reach).astype(held_as)


def setup_inputs(seed: int = 0, part: int = 0) -> dict:
    key_list = jax.random.split(jax.random.key(seed), 13)
    own_keys = jax.random.split(jax.random.fold_in(key_list[12], part), 13)
    return {
        "queries": draw_queries(jax.random.fold_in(jax.random.fold_in(key_list[12], part), 71), part),
        "cache": draw_cache(jax.random.fold_in(jax.random.fold_in(key_list[12], part), 71), part),
        "page_row": draw_page_row(jax.random.fold_in(jax.random.fold_in(key_list[12], part), 71), part),
        "page_index": draw_page_index(jax.random.fold_in(jax.random.fold_in(key_list[12], part), 71), part),
        "lengths": draw_lengths(jax.random.fold_in(jax.random.fold_in(key_list[12], part), 71), part),
        "hidden_in": normal_values(own_keys[5], (ROWS, D), 0.5, 4.0, ((1, 16),)),
        "norm_gain": jnp.clip(1.0 + 0.18 * jax.random.normal(key_list[6], (D,), jnp.float32), 0.1, 1.9),
        "absorb_value": normal_values(key_list[7], (H, LAT, VHEAD), (LAT // 4) ** -0.5, 0.5, ((0, 16),)),
        "out_proj": normal_values(key_list[8], (H * VHEAD, D), (H * VHEAD // 4) ** -0.5, 0.09375, ((0, 16),)),
        "gate_proj": normal_values(key_list[9], (D, FF), D ** -0.5, 0.0625, ((1, 16),)),
        "up_proj": normal_values(key_list[10], (D, FF), D ** -0.5, 0.0625, ((1, 16),)),
        "down_proj": normal_values(key_list[11], (FF, D), (FF // 4) ** -0.5, 0.125, ((0, 16),)),
    }


NEG_BIG = -1e+30
EPS = 1e-06

def merge_pair(first, second):
    joint = jnp.maximum(first[0], second[0])
    factor_a = jnp.exp(first[0] - joint)
    factor_b = jnp.exp(second[0] - joint)
    total = first[1] * factor_a + second[1] * factor_b
    latent = first[2] * factor_a[..., None] + second[2] * factor_b[..., None]
    return (joint, total, latent)

def reference(queries, cache, page_row, page_index, lengths, hidden_in, norm_gain, absorb_value, out_proj, gate_proj, up_proj, down_proj):
    slot_count = PAGES_DEV * PAGE
    softmax_scale = float(VHEAD + ROPE) ** (-0.5)
    cache_shards = cache.reshape(N_CTX, slot_count, ENTRY)
    row_shards = page_row.reshape(N_CTX, PAGES_DEV)
    index_shards = page_index.reshape(N_CTX, PAGES_DEV)
    query_wide = queries.astype(jnp.float32)
    row_ids = jnp.arange(ROWS, dtype=jnp.int32)
    slot_ids = jnp.arange(slot_count, dtype=jnp.int32)

    def shard_step(carry, inputs):
        cache_part, rows_part, index_part = inputs
        row_of = jnp.repeat(rows_part, PAGE)
        position = jnp.repeat(index_part, PAGE) * PAGE + slot_ids % PAGE
        visible = (row_of[None, :] == row_ids[:, None]) & (position[None, :] < lengths[:, None])
        cache_wide = cache_part.astype(jnp.float32)
        scores = jnp.einsum('bhe,te->bht', query_wide, cache_wide) * softmax_scale
        masked = jnp.where(visible[:, None, :], scores, NEG_BIG)
        shard_max = lax.optimization_barrier(jnp.max(masked, axis=2))
        weights = jnp.where(visible[:, None, :], jnp.exp(scores - shard_max[..., None]), 0.0)
        shard_total = lax.optimization_barrier(jnp.sum(weights, axis=2))
        weights_low = weights.astype(jnp.bfloat16).astype(jnp.float32)
        shard_latent = jnp.einsum('bht,tc->bhc', weights_low, cache_wide[:, :LAT])
        return (merge_pair(carry, (shard_max, shard_total, shard_latent)), None)
    start = (jnp.full((ROWS, H), NEG_BIG, jnp.float32), jnp.zeros((ROWS, H), jnp.float32), jnp.zeros((ROWS, H, LAT), jnp.float32))
    merged, unused = lax.scan(shard_step, start, (cache_shards, row_shards, index_shards))
    latent_out = (merged[2] / merged[1][..., None]).astype(jnp.bfloat16)
    value_heads = jnp.einsum('bhc,hcv->bhv', latent_out.astype(jnp.float32), absorb_value.astype(jnp.float32)).astype(jnp.bfloat16)
    flat = value_heads.reshape(ROWS, H * VHEAD)
    stream = hidden_in.astype(jnp.float32) + jnp.dot(flat, out_proj, preferred_element_type=jnp.float32)
    norm_scale = lax.rsqrt(lax.optimization_barrier(jnp.mean(stream * stream, axis=1, keepdims=True)) + EPS)
    normed = (stream * norm_scale * norm_gain).astype(jnp.bfloat16)
    gate_act = jnp.dot(normed, gate_proj, preferred_element_type=jnp.float32)
    up_act = jnp.dot(normed, up_proj, preferred_element_type=jnp.float32)
    activated = (jax.nn.silu(gate_act) * up_act).astype(jnp.bfloat16)
    down_terms = jnp.dot(activated, down_proj, preferred_element_type=jnp.float32)
    return (stream + down_terms).astype(jnp.bfloat16)
```

```python
import jax
import jax.numpy as jnp
from jax import lax
from jax.sharding import PartitionSpec as P

LAT = 512
ROPE = 64
VHEAD = 128
PAGE = 128
LANES = 128


NEG_BIG = -1e30
EPS = 1e-06


def swap(value):
    count = lax.axis_size("ctx")
    return lax.ppermute(value, "ctx", [(i, i ^ 1) for i in range(count)])


def core_groups():
    count = lax.axis_size("ctx")
    return [list(range(core, count, 2)) for core in range(2)]


def exchange(value):
    return lax.all_to_all(value, "ctx", 0, 0, tiled=True, axis_index_groups=core_groups())


def spread(value):
    chips = lax.axis_size("ctx") // 2
    return exchange(jnp.broadcast_to(value[None], (chips,) + value.shape))


def shard_partials(query_rows, cache, visible):
    softmax_scale = float(VHEAD + ROPE) ** (-0.5)
    scores = (
        jnp.einsum("pbhe,te->pbht", query_rows, cache, preferred_element_type=jnp.float32)
        * softmax_scale
    )
    mask = visible[None, :, None, :]
    shard_max = jnp.max(jnp.where(mask, scores, NEG_BIG), axis=3)
    weights = jnp.where(mask, jnp.exp(scores - shard_max[..., None]), 0.0)
    shard_total = jnp.sum(weights, axis=3)
    shard_latent = jnp.einsum(
        "pbht,tc->pbhc",
        weights.astype(jnp.bfloat16),
        cache[:, :LAT],
        preferred_element_type=jnp.float32,
    )
    return (shard_max, shard_total, shard_latent)


def pieces_of(value):
    high = lax.reduce_precision(value, 8, 7)
    middle = lax.reduce_precision(value - high, 8, 7)
    return (high, middle, value - high - middle)


def shards(
    queries,
    cache,
    page_row,
    page_index,
    lengths,
    hidden_in,
    norm_gain,
    absorb_value,
    out_proj,
    gate_proj,
    up_proj,
    down_proj,
):
    row_count, head_count, entry = queries.shape
    count = lax.axis_size("ctx")
    chips = count // 2
    shard_index = lax.axis_index("ctx")
    core = shard_index % 2
    slot_ids = jnp.arange(cache.shape[0], dtype=jnp.int32)
    row_of = jnp.repeat(page_row, PAGE)
    position = jnp.repeat(page_index, PAGE) * PAGE + slot_ids % PAGE
    row_ids = jnp.arange(row_count, dtype=jnp.int32)
    visible = (row_of[None, :] == row_ids[:, None]) & (position[None, :] < lengths[:, None])

    query_own = spread(queries.reshape(row_count * head_count, entry))
    query_other = swap(query_own)
    shape = (chips, row_count, head_count, entry)
    max_other, total_other, latent_other = shard_partials(query_other.reshape(shape), cache, visible)
    max_own, total_own, latent_own = shard_partials(query_own.reshape(shape), cache, visible)
    max_in, total_in = swap(jnp.stack([max_other, total_other]))
    latent_in = swap(latent_other.astype(jnp.bfloat16))
    chip_max = jnp.maximum(max_own, max_in)
    factor_own = jnp.exp(max_own - chip_max)
    factor_in = jnp.exp(max_in - chip_max)
    chip_total = total_own * factor_own + total_in * factor_in
    chip_latent = latent_own * factor_own[..., None] + latent_in * factor_in[..., None]
    stats = jnp.stack(pieces_of(chip_max) + pieces_of(chip_total), axis=-1)
    stats = jnp.pad(stats, ((0, 0), (0, 0), (0, 0), (0, LANES - stats.shape[-1])))
    message = jnp.concatenate([chip_latent, stats], axis=-1).astype(jnp.bfloat16)
    message = message.reshape(chips, row_count * head_count, LAT + LANES)
    pieces = exchange(message).astype(jnp.float32)
    part_max = pieces[..., LAT] + pieces[..., LAT + 1] + pieces[..., LAT + 2]
    part_total = pieces[..., LAT + 3] + pieces[..., LAT + 4] + pieces[..., LAT + 5]
    joint = jnp.max(part_max, axis=0)
    factor = jnp.exp(part_max - joint[None])
    total = jnp.sum(part_total * factor, axis=0)
    latent = jnp.sum(pieces[..., :LAT] * factor[..., None], axis=0)
    latent_out = (latent / total[..., None]).astype(jnp.bfloat16)
    latent_out = latent_out.reshape(row_count, head_count, LAT)
    value_heads = jnp.einsum(
        "bhc,hcv->bhv", latent_out, absorb_value, preferred_element_type=jnp.float32
    ).astype(jnp.bfloat16)
    flat = value_heads.reshape(row_count, head_count * value_heads.shape[2])
    attn_terms = jnp.dot(flat, out_proj, preferred_element_type=jnp.float32)

    width_dev = hidden_in.shape[1]
    width = attn_terms.shape[1]
    col_start = shard_index * width_dev
    own_cols = lax.dynamic_slice_in_dim(attn_terms, col_start, width_dev, 1)
    own_cols = own_cols + hidden_in.astype(jnp.float32)
    attn_terms = lax.dynamic_update_slice_in_dim(attn_terms, own_cols, col_start, 1)
    halves = attn_terms.reshape(row_count, 2, width // 2)
    keep = lax.dynamic_index_in_dim(halves, core, 1, keepdims=False)
    send = lax.dynamic_index_in_dim(halves, 1 - core, 1, keepdims=False)
    chip_terms = (keep + swap(send)).astype(jnp.bfloat16)
    mine = jnp.sum(spread(chip_terms).astype(jnp.float32), axis=0)
    other = swap(mine)
    first = jnp.where(core == 0, mine, other)
    second = jnp.where(core == 0, other, mine)
    stream = jnp.concatenate([first, second], axis=1)

    norm_scale = lax.rsqrt(jnp.mean(stream * stream, axis=1, keepdims=True) + EPS)
    normed = (stream * norm_scale * norm_gain).astype(jnp.bfloat16)
    stream_own = lax.dynamic_slice_in_dim(stream, col_start, width_dev, 1)
    gate_act = jnp.dot(normed, gate_proj, preferred_element_type=jnp.float32)
    up_act = jnp.dot(normed, up_proj, preferred_element_type=jnp.float32)
    activated = (jax.nn.silu(gate_act) * up_act).astype(jnp.bfloat16)
    down_terms = jnp.dot(activated, down_proj, preferred_element_type=jnp.float32)
    blocks = down_terms.reshape(row_count, count, width_dev).swapaxes(0, 1)
    parts = lax.all_to_all(blocks.astype(jnp.bfloat16), "ctx", 0, 0, tiled=True)
    ffn_own = jnp.sum(parts.astype(jnp.float32), axis=0)
    return (stream_own + ffn_own).astype(jnp.bfloat16)


def solution(mesh):
    in_specs = (
        P("groups", "ctx", None),
        P(("groups", "ctx"), None),
        P(("groups", "ctx")),
        P(("groups", "ctx")),
        P("groups"),
        P("groups", "ctx"),
        P(),
        P("ctx", None, None),
        P("ctx", None),
        P(None, "ctx"),
        P(None, "ctx"),
        P("ctx", None),
    )
    out_specs = P("groups", "ctx")
    return jax.shard_map(shards, mesh=mesh, in_specs=in_specs, out_specs=out_specs, check_vma=False)
```

```python
import functools
import math

import jax
import jax.numpy as jnp
from jax import lax
from jax.experimental import pallas as pl
from jax.experimental.pallas import tpu as pltpu
from jax.sharding import PartitionSpec as P

LAT = 512
ROPE = 64
VHEAD = 128
PAGE = 128
LANES = 128
COLUMN_BLOCK = 1792
KERNEL_VMEM = 6 << 20
HINT_FLOPS = 100_000
HINT_TRANSCENDENTALS = 100_000_000


NEG_BIG = -1e30
EPS = 1e-06

VMEM = pl.BlockSpec(memory_space=pltpu.VMEM)
SMEM = pl.BlockSpec(memory_space=pltpu.SMEM)


def swap(value):
    count = lax.axis_size("ctx")
    return lax.ppermute(value, "ctx", [(i, i ^ 1) for i in range(count)])


def core_groups():
    count = lax.axis_size("ctx")
    return [list(range(core, count, 2)) for core in range(2)]


def exchange(value):
    return lax.all_to_all(value, "ctx", 0, 0, tiled=True, axis_index_groups=core_groups())


def spread(value):
    chips = lax.axis_size("ctx") // 2
    return exchange(jnp.broadcast_to(value[None], (chips,) + value.shape))


def call(kernel, out_shape, specs, operands, scratch=(), ahead=()):
    bytes_of = [x.size * x.dtype.itemsize for x in operands]
    flops = HINT_FLOPS * sum(x.size * x.dtype.itemsize for x in ahead)
    return pl.pallas_call(
        kernel,
        out_shape=out_shape,
        in_specs=list(specs),
        out_specs=jax.tree.map(lambda _: VMEM, out_shape),
        scratch_shapes=list(scratch),
        cost_estimate=pl.CostEstimate(
            flops=flops, bytes_accessed=sum(bytes_of), transcendentals=HINT_TRANSCENDENTALS
        ),
        compiler_params=pltpu.CompilerParams(vmem_limit_bytes=KERNEL_VMEM),
    )(*operands)


def as_pieces(value):
    high = value.astype(jnp.bfloat16).astype(jnp.float32)
    rest = value - high
    middle = rest.astype(jnp.bfloat16).astype(jnp.float32)
    return (high, middle, rest - middle)


def copies_kernel(query, copies):
    for chip in range(copies.shape[0]):
        copies[chip] = query[...]


def stats_tile(shard_max, total):
    lane = lax.broadcasted_iota(jnp.int32, (shard_max.shape[0], LANES), 1)
    tile = jnp.zeros(lane.shape, jnp.float32)
    for at, piece in enumerate(as_pieces(shard_max) + as_pieces(total)):
        tile = jnp.where(lane == at, piece, tile)
    return tile.astype(jnp.bfloat16)


def from_stats(tile):
    tile = tile.astype(jnp.float32)
    shard_max = tile[:, 0:1] + tile[:, 1:2] + tile[:, 2:3]
    total = tile[:, 3:4] + tile[:, 4:5] + tile[:, 5:6]
    return (shard_max, total)


def attend(rows, heads, page_row, page_index, lengths, query, cache):
    scale = float(VHEAD + ROPE) ** (-0.5)
    scores = jnp.dot(query[...], cache[...], preferred_element_type=jnp.float32) * scale
    line = lax.broadcasted_iota(jnp.int32, (query.shape[0], PAGE), 0)
    lane = lax.broadcasted_iota(jnp.int32, (query.shape[0], PAGE), 1)
    row_of = lax.rem(lax.div(line, jnp.int32(heads)), jnp.int32(rows))
    visible, blocks = [], []
    for page in range(cache.shape[1] // PAGE):
        owner = page_row[page]
        filled = lengths[owner] - page_index[page] * PAGE
        visible.append((row_of == owner) & (lane < filled))
        blocks.append(scores[:, page * PAGE : (page + 1) * PAGE])
    top = jnp.full((query.shape[0], PAGE), NEG_BIG, jnp.float32)
    for seen, block in zip(visible, blocks):
        top = jnp.maximum(top, jnp.where(seen, block, NEG_BIG))
    shard_max = jnp.max(top, axis=1, keepdims=True)
    weights = [
        jnp.where(seen, jnp.exp(block - shard_max), 0.0) for seen, block in zip(visible, blocks)
    ]
    total = jnp.sum(functools.reduce(jnp.add, weights), axis=1, keepdims=True)
    latent = lax.dot_general(
        jnp.concatenate(weights, axis=1).astype(jnp.bfloat16),
        cache[:LAT, :],
        (((1,), (1,)), ((), ())),
        preferred_element_type=jnp.float32,
    )
    return (shard_max, total, latent)


def send_kernel(rows, heads, page_row, page_index, lengths, query, cache, message):
    shard_max, total, latent = attend(rows, heads, page_row, page_index, lengths, query, cache)
    message[:, :LAT] = latent.astype(jnp.bfloat16)
    message[:, LAT:] = stats_tile(shard_max, total)


def keep_kernel(rows, heads, page_row, page_index, lengths, query, cache, latent_out, stats):
    shard_max, total, latent = attend(rows, heads, page_row, page_index, lengths, query, cache)
    latent_out[...] = latent
    stats[:, :LANES] = jnp.broadcast_to(shard_max, (shard_max.shape[0], LANES))
    stats[:, LANES:] = jnp.broadcast_to(total, (total.shape[0], LANES))


def merge_kernel(latent_own, stats, received, message):
    max_own, total_own = stats[:, 0:1], stats[:, LANES : LANES + 1]
    max_in, total_in = from_stats(received[:, LAT:])
    chip_max = jnp.maximum(max_own, max_in)
    factor_own = jnp.exp(max_own - chip_max)
    factor_in = jnp.exp(max_in - chip_max)
    latent = latent_own[...] * factor_own + received[:, :LAT].astype(jnp.float32) * factor_in
    message[:, :LAT] = latent.astype(jnp.bfloat16)
    message[:, LAT:] = stats_tile(chip_max, total_own * factor_own + total_in * factor_in)


def own_span(width_dev):
    index = lax.axis_index("ctx")
    span = math.lcm(width_dev, LANES)
    start = pl.multiple_of(lax.div(index, span // width_dev) * span, LANES)
    return (start, span, lax.rem(index, span // width_dev))


def heads_kernel(rows, heads, parts, absorb, out_proj, hidden, keep, send, latent_buf):
    chips = parts.shape[0]
    stats = [from_stats(parts[chip, :, LAT:]) for chip in range(chips)]
    joint = functools.reduce(jnp.maximum, [shard_max for shard_max, _ in stats])
    total = jnp.zeros_like(joint)
    latent = jnp.zeros((rows * heads, LAT), jnp.float32)
    for chip, (shard_max, part_total) in enumerate(stats):
        factor = jnp.exp(shard_max - joint)
        total += part_total * factor
        latent += parts[chip, :, :LAT].astype(jnp.float32) * factor
    latent = latent / total
    tiles = range(LAT // LANES)
    for tile in tiles:
        latent_buf[tile] = latent[:, tile * LANES : (tile + 1) * LANES]
    value_heads = []
    for head in range(heads):
        lines = pl.ds(head, rows, stride=heads)
        own = jnp.concatenate([latent_buf[tile, lines, :] for tile in tiles], axis=1)
        own = own.astype(jnp.bfloat16)
        value_heads.append(jnp.dot(own, absorb[head], preferred_element_type=jnp.float32))
    flat = jnp.concatenate(value_heads, axis=1).astype(jnp.bfloat16)
    core = lax.rem(lax.axis_index("ctx"), 2)
    half = keep.shape[1]
    step = math.gcd(half, COLUMN_BLOCK)
    for target, start in ((send, (1 - core) * half), (keep, core * half)):
        for at in range(0, half, step):
            columns = pl.ds(pl.multiple_of(start + at, LANES), step)
            terms = jnp.dot(flat, out_proj[:, columns], preferred_element_type=jnp.float32)
            target[:, at : at + step] = terms
    width_dev = hidden.shape[1]
    start, span, place = own_span(width_dev)
    own = hidden[...].astype(jnp.float32)
    residual = jnp.zeros((rows, span), jnp.float32)
    for at in range(span // width_dev):
        before, after = at * width_dev, span - (at + 1) * width_dev
        pads = [jnp.zeros((rows, size), jnp.float32) for size in (before, after)]
        parts_of = [pads[0]] * (before > 0) + [own] + [pads[1]] * (after > 0)
        residual = jnp.where(place == at, jnp.concatenate(parts_of, axis=1), residual)
    in_half = pl.ds(pl.multiple_of(lax.rem(start, half), LANES), span)
    kept = lax.div(start, half) == core

    @pl.when(kept)
    def _():
        keep[:, in_half] += residual

    @pl.when(jnp.logical_not(kept))
    def _():
        send[:, in_half] += residual


def ffn_kernel(mine, other, gain, gate, up, down, blocks, stream_own):
    rows, half = mine.shape
    width = 2 * half
    core = lax.rem(lax.axis_index("ctx"), 2)
    square = jnp.sum(mine[...] * mine[...], axis=1, keepdims=True)
    square += jnp.sum(other[...] * other[...], axis=1, keepdims=True)
    norm_scale = lax.rsqrt(square / width + EPS)
    step = math.gcd(half, COLUMN_BLOCK)
    gate_act = jnp.zeros((rows, gate.shape[0]), jnp.float32)
    up_act = jnp.zeros((rows, gate.shape[0]), jnp.float32)
    minor = (((1,), (1,)), ((), ()))
    for source, start in ((mine, core * half), (other, (1 - core) * half)):
        for at in range(0, half, step):
            columns = pl.ds(pl.multiple_of(start + at, LANES), step)
            normed = source[:, at : at + step] * norm_scale * gain[:, columns]
            normed = normed.astype(jnp.bfloat16)
            gate_act += lax.dot_general(
                normed, gate[:, columns], minor, preferred_element_type=jnp.float32
            )
            up_act += lax.dot_general(
                normed, up[:, columns], minor, preferred_element_type=jnp.float32
            )
    activated = (gate_act / (1.0 + jnp.exp(-gate_act)) * up_act).astype(jnp.bfloat16)
    count, _, width_dev = blocks.shape
    step = math.lcm(width_dev, LANES)
    for at in range(0, width, step):
        terms = jnp.dot(activated, down[:, at : at + step], preferred_element_type=jnp.float32)
        terms = terms.astype(jnp.bfloat16)
        for inner in range(0, step, width_dev):
            blocks[(at + inner) // width_dev] = terms[:, inner : inner + width_dev]
    start, span, place = own_span(width_dev)
    in_half = pl.ds(pl.multiple_of(lax.rem(start, half), LANES), span)
    near = jnp.where(lax.div(start, half) == core, mine[:, in_half], other[:, in_half])
    own = near[:, :width_dev]
    for at in range(1, span // width_dev):
        own = jnp.where(place == at, near[:, at * width_dev : (at + 1) * width_dev], own)
    stream_own[...] = own


def shards(
    queries,
    cache,
    page_row,
    page_index,
    lengths,
    hidden_in,
    norm_gain,
    absorb_value,
    out_proj,
    gate_proj,
    up_proj,
    down_proj,
):
    rows, heads, entry = queries.shape
    count = lax.axis_size("ctx")
    chips = count // 2
    width_dev = hidden_in.shape[1]
    width = out_proj.shape[1]
    half = width // 2
    lines = rows * heads
    group = chips * lines
    bf16, f32 = jnp.bfloat16, jnp.float32
    shaped = jax.ShapeDtypeStruct

    copies = call(
        copies_kernel,
        shaped((chips, lines, entry), bf16),
        [VMEM],
        (queries.reshape(lines, entry),),
        ahead=(cache, cache),
    )
    query_own = exchange(copies).reshape(group, entry)
    query_other = swap(query_own)
    cache_t = cache.T
    tables = (page_row, page_index, lengths)
    specs = [SMEM, SMEM, SMEM, VMEM, VMEM]
    message = call(
        functools.partial(send_kernel, rows, heads),
        shaped((group, LAT + LANES), bf16),
        specs,
        tables + (query_other, cache_t),
    )
    received = swap(message)
    latent_own, stats = call(
        functools.partial(keep_kernel, rows, heads),
        (shaped((group, LAT), f32), shaped((group, 2 * LANES), f32)),
        specs,
        tables + (query_own, cache_t),
    )
    message = call(
        merge_kernel,
        shaped((group, LAT + LANES), bf16),
        [VMEM] * 3,
        (latent_own, stats, received),
        ahead=(absorb_value, out_proj),
    )
    parts = exchange(message.reshape(chips, lines, LAT + LANES))

    keep, send = call(
        functools.partial(heads_kernel, rows, heads),
        (shaped((rows, half), f32), shaped((rows, half), f32)),
        [VMEM] * 4,
        (parts, absorb_value, out_proj, hidden_in),
        scratch=[pltpu.VMEM((LAT // LANES, lines, LANES), f32)],
        ahead=(gate_proj, up_proj, down_proj),
    )
    chip_terms = (keep + swap(send)).astype(bf16)
    mine = jnp.sum(spread(chip_terms).astype(f32), axis=0)
    other = swap(mine)
    blocks, stream_own = call(
        ffn_kernel,
        (shaped((count, rows, width_dev), bf16), shaped((rows, width_dev), f32)),
        [VMEM] * 6,
        (mine, other, norm_gain[None], gate_proj.T, up_proj.T, down_proj),
    )
    received = lax.all_to_all(blocks, "ctx", 0, 0, tiled=True)
    return (stream_own + jnp.sum(received.astype(f32), axis=0)).astype(bf16)


def solution(mesh):
    in_specs = (
        P("groups", "ctx", None),
        P(("groups", "ctx"), None),
        P(("groups", "ctx")),
        P(("groups", "ctx")),
        P("groups"),
        P("groups", "ctx"),
        P(),
        P("ctx", None, None),
        P("ctx", None),
        P(None, "ctx"),
        P(None, "ctx"),
        P("ctx", None),
    )
    out_specs = P("groups", "ctx")
    return jax.shard_map(shards, mesh=mesh, in_specs=in_specs, out_specs=out_specs, check_vma=False)
```

```python
import functools
import math

import jax
import jax.numpy as jnp
from jax import lax
from jax.experimental import pallas as pl
from jax.experimental.pallas import tpu as pltpu
from jax.sharding import PartitionSpec as P

LAT = 512
ROPE = 64
VHEAD = 128
PAGE = 128
LANES = 128
COLUMN_BLOCK = 1792
KERNEL_VMEM = 12 << 20
HINT_FLOPS = 100_000
HINT_TRANSCENDENTALS = 100_000_000


NEG_BIG = -1e30
EPS = 1e-06

VMEM = pl.BlockSpec(memory_space=pltpu.VMEM)
HBM = pl.BlockSpec(memory_space=pltpu.HBM)


def swap(value):
    count = lax.axis_size("ctx")
    return lax.ppermute(value, "ctx", [(i, i ^ 1) for i in range(count)])


def core_groups():
    count = lax.axis_size("ctx")
    return [list(range(core, count, 2)) for core in range(2)]


def gather_blocks(block):
    count = lax.axis_size("ctx")
    blocks, mask = {0: block}, count // 4
    while mask:
        pairs = [(i, i ^ (2 * mask)) for i in range(count)]
        blocks |= {mask | at: lax.ppermute(held, "ctx", pairs) for at, held in blocks.items()}
        mask //= 2
    return blocks


def exchange(value):
    return lax.all_to_all(value, "ctx", 0, 0, tiled=True, axis_index_groups=core_groups())


def spread(value):
    chips = lax.axis_size("ctx") // 2
    return exchange(jnp.broadcast_to(value[None], (chips,) + value.shape))


def call(kernel, out_shape, specs, operands, scratch=(), ahead=()):
    bytes_of = [x.size * x.dtype.itemsize for x in operands]
    flops = HINT_FLOPS * sum(x.size * x.dtype.itemsize for x in ahead)
    return pl.pallas_call(
        kernel,
        out_shape=out_shape,
        in_specs=list(specs),
        out_specs=jax.tree.map(lambda _: VMEM, out_shape),
        scratch_shapes=list(scratch),
        cost_estimate=pl.CostEstimate(
            flops=flops, bytes_accessed=sum(bytes_of), transcendentals=HINT_TRANSCENDENTALS
        ),
        compiler_params=pltpu.CompilerParams(vmem_limit_bytes=KERNEL_VMEM),
    )(*operands)


def as_pieces(value):
    high = value.astype(jnp.bfloat16).astype(jnp.float32)
    rest = value - high
    middle = rest.astype(jnp.bfloat16).astype(jnp.float32)
    return (high, middle, rest - middle)


def stats_tile(shard_max, total):
    lane = lax.broadcasted_iota(jnp.int32, (shard_max.shape[0], LANES), 1)
    tile = jnp.zeros(lane.shape, jnp.float32)
    for at, piece in enumerate(as_pieces(shard_max) + as_pieces(total)):
        tile = jnp.where(lane == at, piece, tile)
    return tile.astype(jnp.bfloat16)


def from_stats(tile):
    tile = tile.astype(jnp.float32)
    shard_max = tile[:, 0:1] + tile[:, 1:2] + tile[:, 2:3]
    total = tile[:, 3:4] + tile[:, 4:5] + tile[:, 5:6]
    return (shard_max, total)


def first_kernel(mark):
    mark[...] = jnp.zeros_like(mark)


def table_kernel(page_row, page_index, lengths, mark, table, *scratch):
    held, arrived = scratch[:3], scratch[3]
    copies = [
        pltpu.make_async_copy(source, target, arrived.at[at])
        for at, (source, target) in enumerate(zip((page_row, page_index, lengths), held))
    ]
    for copy in copies:
        copy.start()
    for copy in copies:
        copy.wait()
    rows_held, index_held, lengths_held = held
    for page in range(page_row.shape[0]):
        owner = rows_held[page]
        filled = lengths_held[owner] - index_held[page] * PAGE
        table[2 * page : 2 * page + 1] = jnp.full((1, LANES), owner, jnp.int32)
        table[2 * page + 1 : 2 * page + 2] = jnp.full((1, LANES), filled, jnp.int32)


def attend_kernel(rows, heads, masks, tables, queries, own, other, before, message):
    query = jnp.concatenate([block[...] for block in queries], axis=0)
    scale = float(VHEAD + ROPE) ** (-0.5)
    shape = (query.shape[0], PAGE)
    line = lax.broadcasted_iota(jnp.int32, shape, 0)
    lane = lax.broadcasted_iota(jnp.int32, shape, 1)
    row_of = lax.rem(lax.div(line, jnp.int32(heads)), jnp.int32(rows))
    visible, blocks = [], []
    for table, cache in zip(tables, (own, other)):
        scores = jnp.dot(query, cache[...], preferred_element_type=jnp.float32) * scale
        for page in range(cache.shape[1] // PAGE):
            owner, filled = table[2 * page : 2 * page + 1], table[2 * page + 1 : 2 * page + 2]
            visible.append((row_of == owner) & (lane < filled))
            blocks.append(scores[:, page * PAGE : (page + 1) * PAGE])
    top = jnp.full(shape, NEG_BIG, jnp.float32)
    for seen, block in zip(visible, blocks):
        top = jnp.maximum(top, jnp.where(seen, block, NEG_BIG))
    chip_max = jnp.max(top, axis=1, keepdims=True)
    weights = [
        jnp.where(seen, jnp.exp(block - chip_max), 0.0) for seen, block in zip(visible, blocks)
    ]
    total = jnp.sum(functools.reduce(jnp.add, weights), axis=1, keepdims=True)
    latent = jnp.zeros((query.shape[0], LAT), jnp.float32)
    pages = own.shape[1] // PAGE
    for side, cache in enumerate((own, other)):
        low = jnp.concatenate(weights[side * pages : (side + 1) * pages], axis=1)
        latent += lax.dot_general(
            low.astype(jnp.bfloat16),
            cache[:LAT, :],
            (((1,), (1,)), ((), ())),
            preferred_element_type=jnp.float32,
        )
    lines = rows * heads
    stats = stats_tile(chip_max, total)
    latent = latent.astype(jnp.bfloat16)
    chip = lax.div(lax.axis_index("ctx"), 2)
    for at, mask in enumerate(masks):
        target = at if before is None else chip ^ mask
        message[target, :, :LAT] = latent[at * lines : (at + 1) * lines]
        message[target, :, LAT:] = stats[at * lines : (at + 1) * lines]
    if before is not None:
        finished, finished_masks = before
        for at, mask in enumerate(finished_masks):
            message[chip ^ mask] = finished[at]


def near_kernel(rows, heads, masks, *refs):
    tables, queries, (own, other, message) = refs[:2], refs[2:-3], refs[-3:]
    attend_kernel(rows, heads, masks, tables, queries, own, other, None, message)


def far_kernel(rows, heads, masks, near_masks, *refs):
    tables, queries, (own, other, near, message) = refs[:2], refs[2:-4], refs[-4:]
    before = (near, near_masks)
    attend_kernel(rows, heads, masks, tables, queries, own, other, before, message)


def own_span(width_dev):
    index = lax.axis_index("ctx")
    span = math.lcm(width_dev, LANES)
    start = pl.multiple_of(lax.div(index, span // width_dev) * span, LANES)
    return (start, span, lax.rem(index, span // width_dev))


def project(flat, out_proj, start, target):
    step = math.gcd(target.shape[1], COLUMN_BLOCK)
    for at in range(0, target.shape[1], step):
        columns = pl.ds(pl.multiple_of(start + at, LANES), step)
        terms = jnp.dot(flat, out_proj[:, columns], preferred_element_type=jnp.float32)
        target[:, at : at + step] = terms


def add_residual(hidden, wanted, target):
    rows, width_dev = hidden.shape
    half = target.shape[1]
    start, span, place = own_span(width_dev)

    @pl.when(lax.div(start, half) == wanted)
    def _():
        own = hidden[...].astype(jnp.float32)
        residual = jnp.zeros((rows, span), jnp.float32)
        for at in range(span // width_dev):
            before, after = at * width_dev, span - (at + 1) * width_dev
            pieces = [jnp.zeros((rows, before), jnp.float32)] * (before > 0) + [own]
            pieces += [jnp.zeros((rows, after), jnp.float32)] * (after > 0)
            residual = jnp.where(place == at, jnp.concatenate(pieces, axis=1), residual)
        target[:, pl.ds(pl.multiple_of(lax.rem(start, half), LANES), span)] += residual


def heads_kernel(rows, heads, parts, absorb, out_proj, hidden, send, flat_out, latent_buf):
    chips = parts.shape[0]
    stats = [from_stats(parts[chip, :, LAT:]) for chip in range(chips)]
    joint = functools.reduce(jnp.maximum, [shard_max for shard_max, _ in stats])
    total = jnp.zeros_like(joint)
    latent = jnp.zeros((rows * heads, LAT), jnp.float32)
    for chip, (shard_max, part_total) in enumerate(stats):
        factor = jnp.exp(shard_max - joint)
        total += part_total * factor
        latent += parts[chip, :, :LAT].astype(jnp.float32) * factor
    latent = latent / total
    tiles = range(LAT // LANES)
    for tile in tiles:
        latent_buf[tile] = latent[:, tile * LANES : (tile + 1) * LANES]
    value_heads = []
    for head in range(heads):
        lines = pl.ds(head, rows, stride=heads)
        own = jnp.concatenate([latent_buf[tile, lines, :] for tile in tiles], axis=1)
        own = own.astype(jnp.bfloat16)
        value_heads.append(jnp.dot(own, absorb[head], preferred_element_type=jnp.float32))
    flat = jnp.concatenate(value_heads, axis=1).astype(jnp.bfloat16)
    flat_out[...] = flat
    other_core = 1 - lax.rem(lax.axis_index("ctx"), 2)
    project(flat, out_proj, other_core * send.shape[1], send)
    add_residual(hidden, other_core, send)


def keep_kernel(flat, out_proj, hidden, keep):
    core = lax.rem(lax.axis_index("ctx"), 2)
    project(flat[...], out_proj, core * keep.shape[1], keep)
    add_residual(hidden, core, keep)


def expand(side, start, gain, gate, up):
    rows, half = side.shape
    units = gate.shape[0]
    step = math.gcd(half, COLUMN_BLOCK)
    both = jnp.zeros((rows, 2 * units), jnp.float32)
    for at in range(0, half, step):
        columns = pl.ds(pl.multiple_of(start + at, LANES), step)
        scaled = (side[:, at : at + step] * gain[:, columns]).astype(jnp.bfloat16)
        both += lax.dot_general(
            scaled,
            jnp.concatenate([gate[:, columns], up[:, columns]], axis=0),
            (((1,), (1,)), ((), ())),
            preferred_element_type=jnp.float32,
        )
    return both


def own_half_kernel(mine, gain, gate, up, both):
    core = lax.rem(lax.axis_index("ctx"), 2)
    both[...] = expand(mine, core * mine.shape[1], gain, gate, up)


def ffn_kernel(mine, other, both, gain, gate, up, down, blocks, stream_own):
    rows, half = mine.shape
    width, units = 2 * half, gate.shape[0]
    core = lax.rem(lax.axis_index("ctx"), 2)
    square = jnp.sum(mine[...] * mine[...], axis=1, keepdims=True)
    square += jnp.sum(other[...] * other[...], axis=1, keepdims=True)
    norm_scale = lax.rsqrt(square / width + EPS)
    acts = (both[...] + expand(other, (1 - core) * half, gain, gate, up)) * norm_scale
    gate_act, up_act = acts[:, :units], acts[:, units:]
    activated = (gate_act / (1.0 + jnp.exp(-gate_act)) * up_act).astype(jnp.bfloat16)
    count, _, width_dev = blocks.shape
    step = math.lcm(width_dev, LANES)
    for at in range(0, width, step):
        terms = jnp.dot(activated, down[:, at : at + step], preferred_element_type=jnp.float32)
        terms = terms.astype(jnp.bfloat16)
        for inner in range(0, step, width_dev):
            blocks[(at + inner) // width_dev] = terms[:, inner : inner + width_dev]
    start, span, place = own_span(width_dev)
    in_half = pl.ds(pl.multiple_of(lax.rem(start, half), LANES), span)
    near = jnp.where(lax.div(start, half) == core, mine[:, in_half], other[:, in_half])
    own = near[:, :width_dev]
    for at in range(1, span // width_dev):
        own = jnp.where(place == at, near[:, at * width_dev : (at + 1) * width_dev], own)
    stream_own[...] = own


def shards(
    queries,
    cache,
    page_row,
    page_index,
    lengths,
    hidden_in,
    norm_gain,
    absorb_value,
    out_proj,
    gate_proj,
    up_proj,
    down_proj,
):
    rows, heads, entry = queries.shape
    count = lax.axis_size("ctx")
    chips = count // 2
    width_dev = hidden_in.shape[1]
    width = out_proj.shape[1]
    half = width // 2
    lines = rows * heads
    group = chips * lines
    bf16, f32 = jnp.bfloat16, jnp.float32
    shaped = jax.ShapeDtypeStruct

    mark = call(first_kernel, shaped((8, LANES), f32), [], (), ahead=(cache, cache))
    queries, cache_sent, mark = lax.optimization_barrier((queries, cache, mark))
    cache_t = cache.T
    cache_other = swap(cache_sent.T)
    pages = page_row.shape[0]
    table = call(
        table_kernel,
        shaped((2 * pages, LANES), jnp.int32),
        [HBM] * 3 + [VMEM],
        (page_row, page_index, lengths, mark),
        scratch=[
            pltpu.SMEM((pages,), jnp.int32),
            pltpu.SMEM((pages,), jnp.int32),
            pltpu.SMEM((rows,), jnp.int32),
            pltpu.SemaphoreType.DMA((3,)),
        ],
    )
    tables = (table, swap(table))
    blocks = gather_blocks(queries.reshape(lines, entry))
    near_masks = [mask for mask in blocks if mask % 2 == 0]
    far_masks = [mask for mask in blocks if mask % 2 == 1]
    near = call(
        functools.partial(near_kernel, rows, heads, near_masks),
        shaped((len(near_masks), lines, LAT + LANES), bf16),
        [VMEM] * (len(near_masks) + 4),
        tables + tuple(blocks[mask] for mask in near_masks) + (cache_t, cache_other),
    )
    message = call(
        functools.partial(far_kernel, rows, heads, far_masks, near_masks),
        shaped((chips, lines, LAT + LANES), bf16),
        [VMEM] * (len(far_masks) + 5),
        tables + tuple(blocks[mask] for mask in far_masks) + (cache_t, cache_other, near),
        ahead=(absorb_value, out_proj),
    )
    parts = exchange(message)
    send, flat = call(
        functools.partial(heads_kernel, rows, heads),
        (shaped((rows, half), f32), shaped((rows, absorb_value.shape[0] * VHEAD), bf16)),
        [VMEM] * 4,
        (parts, absorb_value, out_proj, hidden_in),
        scratch=[pltpu.VMEM((LAT // LANES, lines, LANES), f32)],
        ahead=(gate_proj, up_proj, down_proj),
    )
    keep = call(
        keep_kernel, shaped((rows, half), f32), [VMEM] * 3, (flat, out_proj, hidden_in)
    )
    chip_terms = (keep + swap(send)).astype(bf16)
    mine = jnp.sum(spread(chip_terms).astype(f32), axis=0)
    other = swap(mine)
    weights = (norm_gain[None], gate_proj.T, up_proj.T)
    both = call(
        own_half_kernel,
        shaped((rows, 2 * gate_proj.shape[1]), f32),
        [VMEM] * 4,
        (mine,) + weights,
    )
    blocks, stream_own = call(
        ffn_kernel,
        (shaped((count, rows, width_dev), bf16), shaped((rows, width_dev), f32)),
        [VMEM] * 7,
        (mine, other, both) + weights + (down_proj,),
    )
    received = lax.all_to_all(blocks, "ctx", 0, 0, tiled=True)
    return (stream_own + jnp.sum(received.astype(f32), axis=0)).astype(bf16)


def solution(mesh):
    in_specs = (
        P("groups", "ctx", None),
        P(("groups", "ctx"), None),
        P(("groups", "ctx")),
        P(("groups", "ctx")),
        P("groups"),
        P("groups", "ctx"),
        P(),
        P("ctx", None, None),
        P("ctx", None),
        P(None, "ctx"),
        P(None, "ctx"),
        P("ctx", None),
    )
    out_specs = P("groups", "ctx")
    return jax.shard_map(shards, mesh=mesh, in_specs=in_specs, out_specs=out_specs, check_vma=False)
```

```python
import functools
import math

import jax
import jax.numpy as jnp
from jax import lax
from jax.experimental import pallas as pl
from jax.experimental.pallas import tpu as pltpu
from jax.sharding import PartitionSpec as P

LAT = 512
ROPE = 64
VHEAD = 128
PAGE = 128
LANES = 128
COLUMN_BLOCK = 1792
KERNEL_VMEM = 12 << 20
HINT_FLOPS = 100_000
HINT_TRANSCENDENTALS = 100_000_000


NEG_BIG = -1e30
EPS = 1e-06

VMEM = pl.BlockSpec(memory_space=pltpu.VMEM)
HBM = pl.BlockSpec(memory_space=pltpu.HBM)


def swap(value):
    count = lax.axis_size("ctx")
    return lax.ppermute(value, "ctx", [(i, i ^ 1) for i in range(count)])


def core_groups():
    count = lax.axis_size("ctx")
    return [list(range(core, count, 2)) for core in range(2)]


def gather_blocks(block, mark):
    count = lax.axis_size("ctx")
    blocks, mask = {0: block}, count // 4
    while mask:
        pairs = [(i, i ^ (2 * mask)) for i in range(count)]
        arrived = {}
        for at, held in blocks.items():
            arrived[mask | at] = lax.ppermute(held, "ctx", pairs)
        blocks |= arrived
        if len(blocks) == 2:
            blocks[mask], mark = lax.optimization_barrier((blocks[mask], mark))
        mask //= 2
    return blocks, mark


def exchange(value):
    return lax.all_to_all(value, "ctx", 0, 0, tiled=True, axis_index_groups=core_groups())


def spread(value):
    chips = lax.axis_size("ctx") // 2
    return exchange(jnp.broadcast_to(value[None], (chips,) + value.shape))


def call(kernel, out_shape, specs, operands, scratch=(), ahead=(), scale=1.0):
    bytes_of = [x.size * x.dtype.itemsize for x in operands]
    flops = HINT_FLOPS * scale * sum(x.size * x.dtype.itemsize for x in ahead)
    return pl.pallas_call(
        kernel,
        out_shape=out_shape,
        in_specs=list(specs),
        out_specs=jax.tree.map(lambda _: VMEM, out_shape),
        scratch_shapes=list(scratch),
        cost_estimate=pl.CostEstimate(
            flops=int(flops), bytes_accessed=sum(bytes_of), transcendentals=int(HINT_TRANSCENDENTALS * scale)
        ),
        compiler_params=pltpu.CompilerParams(vmem_limit_bytes=KERNEL_VMEM),
    )(*operands)


def as_pieces(value):
    high = value.astype(jnp.bfloat16).astype(jnp.float32)
    rest = value - high
    middle = rest.astype(jnp.bfloat16).astype(jnp.float32)
    return (high, middle, rest - middle)


def stats_tile(shard_max, total):
    lane = lax.broadcasted_iota(jnp.int32, (shard_max.shape[0], LANES), 1)
    tile = jnp.zeros(lane.shape, jnp.float32)
    for at, piece in enumerate(as_pieces(shard_max) + as_pieces(total)):
        tile = jnp.where(lane == at, piece, tile)
    return tile.astype(jnp.bfloat16)


def from_stats(tile):
    tile = tile.astype(jnp.float32)
    shard_max = tile[:, 0:1] + tile[:, 1:2] + tile[:, 2:3]
    total = tile[:, 3:4] + tile[:, 4:5] + tile[:, 5:6]
    return (shard_max, total)


def first_kernel(mark):
    mark[...] = jnp.zeros_like(mark)


def table_kernel(page_row, page_index, lengths, mark, table, *scratch):
    held, arrived = scratch[:3], scratch[3]
    copies = [
        pltpu.make_async_copy(source, target, arrived.at[at])
        for at, (source, target) in enumerate(zip((page_row, page_index, lengths), held))
    ]
    for copy in copies:
        copy.start()
    for copy in copies:
        copy.wait()
    rows_held, index_held, lengths_held = held
    for page in range(page_row.shape[0]):
        owner = rows_held[page]
        filled = lengths_held[owner] - index_held[page] * PAGE
        table[2 * page : 2 * page + 1] = jnp.full((1, LANES), owner, jnp.int32)
        table[2 * page + 1 : 2 * page + 2] = jnp.full((1, LANES), filled, jnp.int32)


def attend_kernel(rows, heads, masks, tables, queries, own, other, before, message):
    query = jnp.concatenate([block[...] for block in queries], axis=0)
    scale = float(VHEAD + ROPE) ** (-0.5)
    shape = (query.shape[0], PAGE)
    line = lax.broadcasted_iota(jnp.int32, shape, 0)
    lane = lax.broadcasted_iota(jnp.int32, shape, 1)
    row_of = lax.rem(lax.div(line, jnp.int32(heads)), jnp.int32(rows))
    visible, blocks = [], []
    for table, cache in zip(tables, (own, other)):
        scores = jnp.dot(query, cache[...], preferred_element_type=jnp.float32) * scale
        for page in range(cache.shape[1] // PAGE):
            owner, filled = table[2 * page : 2 * page + 1], table[2 * page + 1 : 2 * page + 2]
            visible.append((row_of == owner) & (lane < filled))
            blocks.append(scores[:, page * PAGE : (page + 1) * PAGE])
    top = jnp.full(shape, NEG_BIG, jnp.float32)
    for seen, block in zip(visible, blocks):
        top = jnp.maximum(top, jnp.where(seen, block, NEG_BIG))
    chip_max = jnp.max(top, axis=1, keepdims=True)
    weights = [
        jnp.where(seen, jnp.exp(block - chip_max), 0.0) for seen, block in zip(visible, blocks)
    ]
    total = jnp.sum(functools.reduce(jnp.add, weights), axis=1, keepdims=True)
    latent = jnp.zeros((query.shape[0], LAT), jnp.float32)
    pages = own.shape[1] // PAGE
    for side, cache in enumerate((own, other)):
        low = jnp.concatenate(weights[side * pages : (side + 1) * pages], axis=1)
        latent += lax.dot_general(
            low.astype(jnp.bfloat16),
            cache[:LAT, :],
            (((1,), (1,)), ((), ())),
            preferred_element_type=jnp.float32,
        )
    lines = rows * heads
    stats = stats_tile(chip_max, total)
    latent = latent.astype(jnp.bfloat16)
    chip = lax.div(lax.axis_index("ctx"), 2)
    for at, mask in enumerate(masks):
        target = at if before is None else chip ^ mask
        message[target, :, :LAT] = latent[at * lines : (at + 1) * lines]
        message[target, :, LAT:] = stats[at * lines : (at + 1) * lines]
    if before is not None:
        finished, finished_masks = before
        for at, mask in enumerate(finished_masks):
            message[chip ^ mask] = finished[at]


def near_kernel(rows, heads, masks, *refs):
    tables, queries, (own, other, message) = refs[:2], refs[2:-3], refs[-3:]
    attend_kernel(rows, heads, masks, tables, queries, own, other, None, message)


def far_kernel(rows, heads, masks, near_masks, *refs):
    tables, queries, (own, other, near, message) = refs[:2], refs[2:-4], refs[-4:]
    before = (near, near_masks)
    attend_kernel(rows, heads, masks, tables, queries, own, other, before, message)


def own_span(width_dev):
    index = lax.axis_index("ctx")
    span = math.lcm(width_dev, LANES)
    start = pl.multiple_of(lax.div(index, span // width_dev) * span, LANES)
    return (start, span, lax.rem(index, span // width_dev))


def project(flat, out_proj, start, target):
    step = math.gcd(target.shape[1], COLUMN_BLOCK)
    for at in range(0, target.shape[1], step):
        columns = pl.ds(pl.multiple_of(start + at, LANES), step)
        terms = jnp.dot(flat, out_proj[:, columns], preferred_element_type=jnp.float32)
        target[:, at : at + step] = terms


def add_residual(hidden, wanted, target):
    rows, width_dev = hidden.shape
    half = target.shape[1]
    start, span, place = own_span(width_dev)

    @pl.when(lax.div(start, half) == wanted)
    def _():
        own = hidden[...].astype(jnp.float32)
        residual = jnp.zeros((rows, span), jnp.float32)
        for at in range(span // width_dev):
            before, after = at * width_dev, span - (at + 1) * width_dev
            pieces = [jnp.zeros((rows, before), jnp.float32)] * (before > 0) + [own]
            pieces += [jnp.zeros((rows, after), jnp.float32)] * (after > 0)
            residual = jnp.where(place == at, jnp.concatenate(pieces, axis=1), residual)
        target[:, pl.ds(pl.multiple_of(lax.rem(start, half), LANES), span)] += residual


def heads_kernel(rows, heads, parts, absorb, out_proj, hidden, send, flat_out, latent_buf):
    chips = parts.shape[0]
    stats = [from_stats(parts[chip, :, LAT:]) for chip in range(chips)]
    joint = functools.reduce(jnp.maximum, [shard_max for shard_max, _ in stats])
    total = jnp.zeros_like(joint)
    latent = jnp.zeros((rows * heads, LAT), jnp.float32)
    for chip, (shard_max, part_total) in enumerate(stats):
        factor = jnp.exp(shard_max - joint)
        total += part_total * factor
        latent += parts[chip, :, :LAT].astype(jnp.float32) * factor
    latent = latent / total
    tiles = range(LAT // LANES)
    for tile in tiles:
        latent_buf[tile] = latent[:, tile * LANES : (tile + 1) * LANES]
    value_heads = []
    for head in range(heads):
        lines = pl.ds(head, rows, stride=heads)
        own = jnp.concatenate([latent_buf[tile, lines, :] for tile in tiles], axis=1)
        own = own.astype(jnp.bfloat16)
        value_heads.append(jnp.dot(own, absorb[head], preferred_element_type=jnp.float32))
    flat = jnp.concatenate(value_heads, axis=1).astype(jnp.bfloat16)
    flat_out[...] = flat
    other_core = 1 - lax.rem(lax.axis_index("ctx"), 2)
    project(flat, out_proj, other_core * send.shape[1], send)
    add_residual(hidden, other_core, send)


def keep_kernel(flat, out_proj, hidden, keep):
    core = lax.rem(lax.axis_index("ctx"), 2)
    project(flat[...], out_proj, core * keep.shape[1], keep)
    add_residual(hidden, core, keep)


def expand(side, start, gain, gate, up):
    rows, half = side.shape
    units = gate.shape[0]
    step = math.gcd(half, COLUMN_BLOCK)
    both = jnp.zeros((rows, 2 * units), jnp.float32)
    for at in range(0, half, step):
        columns = pl.ds(pl.multiple_of(start + at, LANES), step)
        scaled = (side[:, at : at + step] * gain[:, columns]).astype(jnp.bfloat16)
        both += lax.dot_general(
            scaled,
            jnp.concatenate([gate[:, columns], up[:, columns]], axis=0),
            (((1,), (1,)), ((), ())),
            preferred_element_type=jnp.float32,
        )
    return both


def own_half_kernel(mine, gain, gate, up, both):
    core = lax.rem(lax.axis_index("ctx"), 2)
    both[...] = expand(mine, core * mine.shape[1], gain, gate, up)


def ffn_kernel(mine, other, both, gain, gate, up, down, blocks, stream_own):
    _, half = mine.shape
    width, units = 2 * half, gate.shape[0]
    core = lax.rem(lax.axis_index("ctx"), 2)
    square = jnp.sum(mine[...] * mine[...], axis=1, keepdims=True)
    square += jnp.sum(other[...] * other[...], axis=1, keepdims=True)
    norm_scale = lax.rsqrt(square / width + EPS)
    acts = (both[...] + expand(other, (1 - core) * half, gain, gate, up)) * norm_scale
    gate_act, up_act = acts[:, :units], acts[:, units:]
    activated = (gate_act / (1.0 + jnp.exp(-gate_act)) * up_act).astype(jnp.bfloat16)
    _, _, width_dev = blocks.shape
    step = math.lcm(width_dev, LANES)
    for at in range(0, width, step):
        terms = jnp.dot(activated, down[:, at : at + step], preferred_element_type=jnp.float32)
        terms = terms.astype(jnp.bfloat16)
        for inner in range(0, step, width_dev):
            blocks[(at + inner) // width_dev] = terms[:, inner : inner + width_dev]
    start, span, place = own_span(width_dev)
    in_half = pl.ds(pl.multiple_of(lax.rem(start, half), LANES), span)
    near = jnp.where(lax.div(start, half) == core, mine[:, in_half], other[:, in_half])
    own = near[:, :width_dev]
    for at in range(1, span // width_dev):
        own = jnp.where(place == at, near[:, at * width_dev : (at + 1) * width_dev], own)
    stream_own[...] = own


def shards(
    queries,
    cache,
    page_row,
    page_index,
    lengths,
    hidden_in,
    norm_gain,
    absorb_value,
    out_proj,
    gate_proj,
    up_proj,
    down_proj,
):
    rows, heads, entry = queries.shape
    count = lax.axis_size("ctx")
    chips = count // 2
    width_dev = hidden_in.shape[1]
    width = out_proj.shape[1]
    half = width // 2
    lines = rows * heads
    bf16, f32 = jnp.bfloat16, jnp.float32
    shaped = jax.ShapeDtypeStruct

    mark = call(first_kernel, shaped((8, LANES), f32), [], (), ahead=(cache, cache), scale=0.1)
    blocks, mark = gather_blocks(queries.reshape(lines, entry), mark)
    cache_sent, mark = lax.optimization_barrier((cache, mark))
    cache_t = cache.T
    cache_other = swap(cache_sent.T)
    pages = page_row.shape[0]
    table = call(
        table_kernel,
        shaped((2 * pages, LANES), jnp.int32),
        [HBM] * 3 + [VMEM],
        (page_row, page_index, lengths, mark),
        scratch=[
            pltpu.SMEM((pages,), jnp.int32),
            pltpu.SMEM((pages,), jnp.int32),
            pltpu.SMEM((rows,), jnp.int32),
            pltpu.SemaphoreType.DMA((3,)),
        ],
    )
    tables = (table, swap(table))
    near_masks = [mask for mask in blocks if mask % 2 == 0]
    far_masks = [mask for mask in blocks if mask % 2 == 1]
    near = call(
        functools.partial(near_kernel, rows, heads, near_masks),
        shaped((len(near_masks), lines, LAT + LANES), bf16),
        [VMEM] * (len(near_masks) + 4),
        tables + tuple(blocks[mask] for mask in near_masks) + (cache_t, cache_other),
    )
    message = call(
        functools.partial(far_kernel, rows, heads, far_masks, near_masks),
        shaped((chips, lines, LAT + LANES), bf16),
        [VMEM] * (len(far_masks) + 5),
        tables + tuple(blocks[mask] for mask in far_masks) + (cache_t, cache_other, near),
        ahead=(absorb_value, out_proj),
    )
    parts = exchange(message)
    send, flat = call(
        functools.partial(heads_kernel, rows, heads),
        (shaped((rows, half), f32), shaped((rows, absorb_value.shape[0] * VHEAD), bf16)),
        [VMEM] * 4,
        (parts, absorb_value, out_proj, hidden_in),
        scratch=[pltpu.VMEM((LAT // LANES, lines, LANES), f32)],
        ahead=(gate_proj, up_proj, down_proj),
    )
    keep = call(
        keep_kernel, shaped((rows, half), f32), [VMEM] * 3, (flat, out_proj, hidden_in)
    )
    chip_terms = (keep + swap(send)).astype(bf16)
    mine = jnp.sum(spread(chip_terms).astype(f32), axis=0)
    other = swap(mine)
    weights = (norm_gain[None], gate_proj.T, up_proj.T)
    both = call(
        own_half_kernel,
        shaped((rows, 2 * gate_proj.shape[1]), f32),
        [VMEM] * 4,
        (mine,) + weights,
    )
    blocks, stream_own = call(
        ffn_kernel,
        (shaped((count, rows, width_dev), bf16), shaped((rows, width_dev), f32)),
        [VMEM] * 7,
        (mine, other, both) + weights + (down_proj,),
    )
    received = lax.all_to_all(blocks, "ctx", 0, 0, tiled=True)
    return (stream_own + jnp.sum(received.astype(f32), axis=0)).astype(bf16)


def solution(mesh):
    in_specs = (
        P("groups", "ctx", None),
        P(("groups", "ctx"), None),
        P(("groups", "ctx")),
        P(("groups", "ctx")),
        P("groups"),
        P("groups", "ctx"),
        P(),
        P("ctx", None, None),
        P("ctx", None),
        P(None, "ctx"),
        P(None, "ctx"),
        P("ctx", None),
    )
    out_specs = P("groups", "ctx")
    return jax.shard_map(shards, mesh=mesh, in_specs=in_specs, out_specs=out_specs, check_vma=False)
```

```python
import functools
import math

import jax
import jax.numpy as jnp
from jax import lax
from jax.experimental import pallas as pl
from jax.experimental.pallas import tpu as pltpu
from jax.sharding import PartitionSpec as P

LAT = 512
ROPE = 64
VHEAD = 128
PAGE = 128
LANES = 128
COLUMN_BLOCK = 1792
STATS = 16
KERNEL_VMEM = 12 << 20
HINT_FLOPS = 100_000
HINT_TRANSCENDENTALS = 100_000_000


NEG_BIG = -1e30
EPS = 1e-06

VMEM = pl.BlockSpec(memory_space=pltpu.VMEM)


def swap(value):
    count = lax.axis_size("ctx")
    return lax.ppermute(value, "ctx", [(i, i ^ 1) for i in range(count)])


def core_groups():
    count = lax.axis_size("ctx")
    return [list(range(core, count, 2)) for core in range(2)]


def gather_blocks(block, mark):
    count = lax.axis_size("ctx")
    blocks, mask = {0: block}, count // 4
    while mask:
        pairs = [(i, i ^ (2 * mask)) for i in range(count)]
        arrived = {}
        for at, held in blocks.items():
            arrived[mask | at] = lax.ppermute(held, "ctx", pairs)
        blocks |= arrived
        if len(blocks) == 2:
            blocks[mask], mark = lax.optimization_barrier((blocks[mask], mark))
        mask //= 2
    return blocks, mark


def exchange(value):
    return lax.all_to_all(value, "ctx", 0, 0, tiled=True, axis_index_groups=core_groups())


def spread(value):
    chips = lax.axis_size("ctx") // 2
    return exchange(jnp.broadcast_to(value[None], (chips,) + value.shape))


def call(kernel, out_shape, specs, operands, scratch=(), ahead=(), scale=1.0):
    bytes_of = [x.size * x.dtype.itemsize for x in operands]
    flops = HINT_FLOPS * scale * sum(x.size * x.dtype.itemsize for x in ahead)
    return pl.pallas_call(
        kernel,
        out_shape=out_shape,
        in_specs=list(specs),
        out_specs=jax.tree.map(lambda _: VMEM, out_shape),
        scratch_shapes=list(scratch),
        cost_estimate=pl.CostEstimate(
            flops=int(flops), bytes_accessed=sum(bytes_of), transcendentals=int(HINT_TRANSCENDENTALS * scale)
        ),
        compiler_params=pltpu.CompilerParams(vmem_limit_bytes=KERNEL_VMEM),
    )(*operands)


def as_pieces(value):
    high = value.astype(jnp.bfloat16).astype(jnp.float32)
    rest = value - high
    middle = rest.astype(jnp.bfloat16).astype(jnp.float32)
    return (high, middle, rest - middle)


def stats_tile(shard_max, total):
    lane = lax.broadcasted_iota(jnp.int32, (shard_max.shape[0], LANES), 1)
    tile = jnp.zeros(lane.shape, jnp.float32)
    for at, piece in enumerate(as_pieces(shard_max) + as_pieces(total)):
        tile = jnp.where(lane == at, piece, tile)
    return tile


def from_stats(tile):
    tile = tile.astype(jnp.float32)
    shard_max = tile[:, 0:1] + tile[:, 1:2] + tile[:, 2:3]
    total = tile[:, 3:4] + tile[:, 4:5] + tile[:, 5:6]
    return (shard_max, total)


def first_kernel(mark):
    mark[...] = jnp.zeros_like(mark)


def table_kernel(page_row, page_index, lengths, mark, table):
    for page in range(page_row.shape[1]):
        owner = page_row[:, page : page + 1]
        filled = page_index[:, page : page + 1] * -PAGE
        for row in range(lengths.shape[1]):
            filled += jnp.where(owner == row, lengths[:, row : row + 1], 0)
        table[2 * page : 2 * page + 1] = jnp.broadcast_to(owner, (1, LANES))
        table[2 * page + 1 : 2 * page + 2] = jnp.broadcast_to(filled, (1, LANES))


def attend_kernel(rows, heads, masks, tables, queries, own, other, before, message):
    query = jnp.concatenate([block[...] for block in queries], axis=0)
    scale = float(VHEAD + ROPE) ** (-0.5)
    shape = (query.shape[0], PAGE)
    line = lax.broadcasted_iota(jnp.int32, shape, 0)
    lane = lax.broadcasted_iota(jnp.int32, shape, 1)
    row_of = lax.rem(lax.div(line, jnp.int32(heads)), jnp.int32(rows))
    visible, blocks = [], []
    for table, cache in zip(tables, (own, other)):
        scores = jnp.dot(query, cache[...], preferred_element_type=jnp.float32) * scale
        for page in range(cache.shape[1] // PAGE):
            owner, filled = table[2 * page : 2 * page + 1], table[2 * page + 1 : 2 * page + 2]
            visible.append((row_of == owner) & (lane < filled))
            blocks.append(scores[:, page * PAGE : (page + 1) * PAGE])
    top = jnp.full(shape, NEG_BIG, jnp.float32)
    for seen, block in zip(visible, blocks):
        top = jnp.maximum(top, jnp.where(seen, block, NEG_BIG))
    chip_max = jnp.max(top, axis=1, keepdims=True)
    weights = [
        jnp.where(seen, jnp.exp(block - chip_max), 0.0) for seen, block in zip(visible, blocks)
    ]
    total = jnp.sum(functools.reduce(jnp.add, weights), axis=1, keepdims=True)
    latent = jnp.zeros((query.shape[0], LAT), jnp.float32)
    pages = own.shape[1] // PAGE
    for side, cache in enumerate((own, other)):
        low = jnp.concatenate(weights[side * pages : (side + 1) * pages], axis=1)
        latent += lax.dot_general(
            low.astype(jnp.bfloat16),
            cache[:LAT, :],
            (((1,), (1,)), ((), ())),
            preferred_element_type=jnp.float32,
        )
    lines = rows * heads
    stats = stats_tile(chip_max, total).T[:STATS].astype(jnp.bfloat16)
    latent = latent.astype(jnp.bfloat16)
    chip = lax.div(lax.axis_index("ctx"), 2)
    for at, mask in enumerate(masks):
        target = at if before is None else chip ^ mask
        for tile in range(LAT // LANES):
            columns = slice(tile * LANES, (tile + 1) * LANES)
            block = latent[at * lines : (at + 1) * lines, columns]
            message[target, tile * lines : (tile + 1) * lines] = block
        message[target, LAT // LANES * lines :] = stats
    if before is not None:
        finished, finished_masks = before
        for at, mask in enumerate(finished_masks):
            message[chip ^ mask] = finished[at]


def near_kernel(rows, heads, masks, *refs):
    tables, queries, (own, other, message) = refs[:2], refs[2:-3], refs[-3:]
    attend_kernel(rows, heads, masks, tables, queries, own, other, None, message)


def far_kernel(rows, heads, masks, near_masks, *refs):
    tables, queries, (own, other, near, message) = refs[:2], refs[2:-4], refs[-4:]
    before = (near, near_masks)
    attend_kernel(rows, heads, masks, tables, queries, own, other, before, message)


def own_span(width_dev):
    index = lax.axis_index("ctx")
    span = math.lcm(width_dev, LANES)
    start = pl.multiple_of(lax.div(index, span // width_dev) * span, LANES)
    return (start, span, lax.rem(index, span // width_dev))


def project(flat, out_proj, start, target):
    step = math.gcd(target.shape[1], COLUMN_BLOCK)
    for at in range(0, target.shape[1], step):
        columns = pl.ds(pl.multiple_of(start + at, LANES), step)
        terms = jnp.dot(flat, out_proj[:, columns], preferred_element_type=jnp.float32)
        target[:, at : at + step] = terms


def add_residual(hidden, wanted, target):
    rows, width_dev = hidden.shape
    half = target.shape[1]
    start, span, place = own_span(width_dev)

    @pl.when(lax.div(start, half) == wanted)
    def _():
        own = hidden[...].astype(jnp.float32)
        residual = jnp.zeros((rows, span), jnp.float32)
        for at in range(span // width_dev):
            before, after = at * width_dev, span - (at + 1) * width_dev
            pieces = [jnp.zeros((rows, before), jnp.float32)] * (before > 0) + [own]
            pieces += [jnp.zeros((rows, after), jnp.float32)] * (after > 0)
            residual = jnp.where(place == at, jnp.concatenate(pieces, axis=1), residual)
        target[:, pl.ds(pl.multiple_of(lax.rem(start, half), LANES), span)] += residual


def heads_kernel(
    rows, heads, orders, parts, absorb, out_proj, hidden, send, flat_out, latent_buf, stats_buf
):
    chips, lines = parts.shape[0], rows * heads
    tiles = range(LAT // LANES)
    last = LAT // LANES * lines
    gathered = [parts[chip, last:].astype(jnp.float32) for chip in range(chips)]
    stats_buf[...] = jnp.concatenate(gathered, axis=0).T
    own_chip = lax.div(lax.axis_index("ctx"), 2)
    stats = []
    for chip in range(chips):
        mask = chip ^ own_chip
        place = jnp.int32(0)
        for order in orders:
            for at, held in enumerate(order):
                place = jnp.where(mask == held, at, place)
        block = stats_buf[pl.ds(pl.multiple_of(place * lines, 8), lines), :]
        stats.append(from_stats(block[:, chip * STATS : (chip + 1) * STATS]))
    joint = functools.reduce(jnp.maximum, [shard_max for shard_max, _ in stats])
    factors = [jnp.exp(shard_max - joint) for shard_max, _ in stats]
    total = sum(part_total * factor for (_, part_total), factor in zip(stats, factors))
    for tile in tiles:
        latent = jnp.zeros((lines, LANES), jnp.float32)
        for chip, factor in enumerate(factors):
            part = parts[chip, tile * lines : (tile + 1) * lines]
            latent += part.astype(jnp.float32) * factor
        latent_buf[tile] = latent / total
    value_heads = []
    for head in range(heads):
        picked = pl.ds(head, rows, stride=heads)
        own = jnp.concatenate([latent_buf[tile, picked, :] for tile in tiles], axis=1)
        own = own.astype(jnp.bfloat16)
        value_heads.append(jnp.dot(own, absorb[head], preferred_element_type=jnp.float32))
    flat = jnp.concatenate(value_heads, axis=1).astype(jnp.bfloat16)
    flat_out[...] = flat
    other_core = 1 - lax.rem(lax.axis_index("ctx"), 2)
    project(flat, out_proj, other_core * send.shape[1], send)
    add_residual(hidden, other_core, send)


def keep_kernel(flat, out_proj, hidden, keep):
    core = lax.rem(lax.axis_index("ctx"), 2)
    project(flat[...], out_proj, core * keep.shape[1], keep)
    add_residual(hidden, core, keep)


def expand(side, start, gain, gate, up):
    rows, half = side.shape
    units = gate.shape[0]
    step = math.gcd(half, COLUMN_BLOCK)
    both = jnp.zeros((rows, 2 * units), jnp.float32)
    for at in range(0, half, step):
        columns = pl.ds(pl.multiple_of(start + at, LANES), step)
        scaled = (side[:, at : at + step] * gain[:, columns]).astype(jnp.bfloat16)
        both += lax.dot_general(
            scaled,
            jnp.concatenate([gate[:, columns], up[:, columns]], axis=0),
            (((1,), (1,)), ((), ())),
            preferred_element_type=jnp.float32,
        )
    return both


def own_half_kernel(mine, gain, gate, up, both):
    core = lax.rem(lax.axis_index("ctx"), 2)
    both[...] = expand(mine, core * mine.shape[1], gain, gate, up)


def ffn_kernel(mine, other, both, gain, gate, up, down, blocks, stream_own):
    _, half = mine.shape
    width, units = 2 * half, gate.shape[0]
    core = lax.rem(lax.axis_index("ctx"), 2)
    square = jnp.sum(mine[...] * mine[...], axis=1, keepdims=True)
    square += jnp.sum(other[...] * other[...], axis=1, keepdims=True)
    norm_scale = lax.rsqrt(square / width + EPS)
    acts = (both[...] + expand(other, (1 - core) * half, gain, gate, up)) * norm_scale
    gate_act, up_act = acts[:, :units], acts[:, units:]
    activated = (gate_act / (1.0 + jnp.exp(-gate_act)) * up_act).astype(jnp.bfloat16)
    _, _, width_dev = blocks.shape
    step = math.lcm(width_dev, LANES)
    for at in range(0, width, step):
        terms = jnp.dot(activated, down[:, at : at + step], preferred_element_type=jnp.float32)
        terms = terms.astype(jnp.bfloat16)
        for inner in range(0, step, width_dev):
            blocks[(at + inner) // width_dev] = terms[:, inner : inner + width_dev]
    start, span, place = own_span(width_dev)
    in_half = pl.ds(pl.multiple_of(lax.rem(start, half), LANES), span)
    near = jnp.where(lax.div(start, half) == core, mine[:, in_half], other[:, in_half])
    own = near[:, :width_dev]
    for at in range(1, span // width_dev):
        own = jnp.where(place == at, near[:, at * width_dev : (at + 1) * width_dev], own)
    stream_own[...] = own


def shards(
    queries,
    cache,
    page_row,
    page_index,
    lengths,
    hidden_in,
    norm_gain,
    absorb_value,
    out_proj,
    gate_proj,
    up_proj,
    down_proj,
):
    rows, heads, entry = queries.shape
    count = lax.axis_size("ctx")
    chips = count // 2
    width_dev = hidden_in.shape[1]
    width = out_proj.shape[1]
    half = width // 2
    lines = rows * heads
    bf16, f32 = jnp.bfloat16, jnp.float32
    shaped = jax.ShapeDtypeStruct

    mark = call(first_kernel, shaped((8, LANES), f32), [], (), ahead=(cache, cache), scale=0.1)
    blocks, mark = gather_blocks(queries.reshape(lines, entry), mark)
    cache_sent, mark = lax.optimization_barrier((cache, mark))
    cache_t = cache.T
    cache_other = swap(cache_sent.T)
    pages = page_row.shape[0]
    table = call(
        table_kernel,
        shaped((2 * pages, LANES), jnp.int32),
        [VMEM] * 4,
        (page_row[None], page_index[None], lengths[None], mark),
    )
    tables = (table, swap(table))
    near_masks = [mask for mask in blocks if mask % 2 == 0]
    far_masks = [mask for mask in blocks if mask % 2 == 1]
    block_shape = (LAT // LANES * lines + STATS, LANES)
    near = call(
        functools.partial(near_kernel, rows, heads, near_masks),
        shaped((len(near_masks),) + block_shape, bf16),
        [VMEM] * (len(near_masks) + 4),
        tables + tuple(blocks[mask] for mask in near_masks) + (cache_t, cache_other),
    )
    message = call(
        functools.partial(far_kernel, rows, heads, far_masks, near_masks),
        shaped((chips,) + block_shape, bf16),
        [VMEM] * (len(far_masks) + 5),
        tables + tuple(blocks[mask] for mask in far_masks) + (cache_t, cache_other, near),
        ahead=(absorb_value, out_proj),
    )
    parts = exchange(message)
    send, flat = call(
        functools.partial(heads_kernel, rows, heads, (near_masks, far_masks)),
        (shaped((rows, half), f32), shaped((rows, absorb_value.shape[0] * VHEAD), bf16)),
        [VMEM] * 4,
        (parts, absorb_value, out_proj, hidden_in),
        scratch=[
            pltpu.VMEM((LAT // LANES, lines, LANES), f32),
            pltpu.VMEM((LANES, chips * STATS), f32),
        ],
        ahead=(gate_proj, up_proj, down_proj),
    )
    keep = call(
        keep_kernel, shaped((rows, half), f32), [VMEM] * 3, (flat, out_proj, hidden_in)
    )
    chip_terms = (keep + swap(send)).astype(bf16)
    mine = jnp.sum(spread(chip_terms).astype(f32), axis=0)
    other = swap(mine)
    weights = (norm_gain[None], gate_proj.T, up_proj.T)
    both = call(
        own_half_kernel,
        shaped((rows, 2 * gate_proj.shape[1]), f32),
        [VMEM] * 4,
        (mine,) + weights,
    )
    blocks, stream_own = call(
        ffn_kernel,
        (shaped((count, rows, width_dev), bf16), shaped((rows, width_dev), f32)),
        [VMEM] * 7,
        (mine, other, both) + weights + (down_proj,),
    )
    received = lax.all_to_all(blocks, "ctx", 0, 0, tiled=True)
    return (stream_own + jnp.sum(received.astype(f32), axis=0)).astype(bf16)


def solution(mesh):
    in_specs = (
        P("groups", "ctx", None),
        P(("groups", "ctx"), None),
        P(("groups", "ctx")),
        P(("groups", "ctx")),
        P("groups"),
        P("groups", "ctx"),
        P(),
        P("ctx", None, None),
        P("ctx", None),
        P(None, "ctx"),
        P(None, "ctx"),
        P("ctx", None),
    )
    out_specs = P("groups", "ctx")
    return jax.shard_map(shards, mesh=mesh, in_specs=in_specs, out_specs=out_specs, check_vma=False)
```

```python
import functools
import math

import jax
import jax.numpy as jnp
from jax import lax
from jax.experimental import pallas as pl
from jax.experimental.pallas import tpu as pltpu
from jax.sharding import PartitionSpec as P

LAT = 512
ROPE = 64
VHEAD = 128
PAGE = 128
LANES = 128
COLUMN_BLOCK = 1792
STATS = 16
KERNEL_VMEM = 12 << 20
HINT_FLOPS = 100_000
HINT_TRANSCENDENTALS = 100_000_000


NEG_BIG = -1e30
EPS = 1e-06

VMEM = pl.BlockSpec(memory_space=pltpu.VMEM)


def swap(value):
    count = lax.axis_size("ctx")
    return lax.ppermute(value, "ctx", [(i, i ^ 1) for i in range(count)])


def core_groups():
    count = lax.axis_size("ctx")
    return [list(range(core, count, 2)) for core in range(2)]


def gather_blocks(block, mark):
    count = lax.axis_size("ctx")
    blocks, mask = {0: block}, count // 4
    while mask:
        pairs = [(i, i ^ (2 * mask)) for i in range(count)]
        arrived = {}
        for at, held in blocks.items():
            arrived[mask | at] = lax.ppermute(held, "ctx", pairs)
        blocks |= arrived
        if len(blocks) == 2:
            blocks[mask], mark = lax.optimization_barrier((blocks[mask], mark))
        mask //= 2
    return blocks, mark


def exchange(value):
    return lax.all_to_all(value, "ctx", 0, 0, tiled=True, axis_index_groups=core_groups())


def spread(value):
    chips = lax.axis_size("ctx") // 2
    return exchange(jnp.broadcast_to(value[None], (chips,) + value.shape))


def call(kernel, out_shape, specs, operands, scratch=(), ahead=(), scale=1.0):
    bytes_of = [x.size * x.dtype.itemsize for x in operands]
    flops = HINT_FLOPS * scale * sum(x.size * x.dtype.itemsize for x in ahead)
    return pl.pallas_call(
        kernel,
        out_shape=out_shape,
        in_specs=list(specs),
        out_specs=jax.tree.map(lambda _: VMEM, out_shape),
        scratch_shapes=list(scratch),
        cost_estimate=pl.CostEstimate(
            flops=int(flops), bytes_accessed=sum(bytes_of), transcendentals=int(HINT_TRANSCENDENTALS * scale)
        ),
        compiler_params=pltpu.CompilerParams(vmem_limit_bytes=KERNEL_VMEM),
    )(*operands)


def as_pieces(value):
    high = value.astype(jnp.bfloat16).astype(jnp.float32)
    rest = value - high
    middle = rest.astype(jnp.bfloat16).astype(jnp.float32)
    return (high, middle, rest - middle)


def stats_tile(shard_max, total):
    lane = lax.broadcasted_iota(jnp.int32, (shard_max.shape[0], LANES), 1)
    tile = jnp.zeros(lane.shape, jnp.float32)
    for at, piece in enumerate(as_pieces(shard_max) + as_pieces(total)):
        tile = jnp.where(lane == at, piece, tile)
    return tile


def from_stats(tile):
    tile = tile.astype(jnp.float32)
    shard_max = tile[:, 0:1] + tile[:, 1:2] + tile[:, 2:3]
    total = tile[:, 3:4] + tile[:, 4:5] + tile[:, 5:6]
    return (shard_max, total)


def first_kernel(mark):
    mark[...] = jnp.zeros_like(mark)


def table_kernel(page_row, page_index, lengths, mark, table):
    for page in range(page_row.shape[1]):
        owner = page_row[:, page : page + 1]
        filled = page_index[:, page : page + 1] * -PAGE
        for row in range(lengths.shape[1]):
            filled += jnp.where(owner == row, lengths[:, row : row + 1], 0)
        table[2 * page : 2 * page + 1] = jnp.broadcast_to(owner, (1, LANES))
        table[2 * page + 1 : 2 * page + 2] = jnp.broadcast_to(filled, (1, LANES))


def attend_kernel(rows, heads, masks, tables, queries, own, other, before, message):
    query = jnp.concatenate([block[...] for block in queries], axis=0)
    scale = float(VHEAD + ROPE) ** (-0.5)
    shape = (query.shape[0], PAGE)
    line = lax.broadcasted_iota(jnp.int32, shape, 0)
    lane = lax.broadcasted_iota(jnp.int32, shape, 1)
    row_of = lax.rem(lax.div(line, jnp.int32(heads)), jnp.int32(rows))
    visible, blocks = [], []
    for table, cache in zip(tables, (own, other)):
        scores = jnp.dot(query, cache[...], preferred_element_type=jnp.float32) * scale
        for page in range(cache.shape[1] // PAGE):
            owner, filled = table[2 * page : 2 * page + 1], table[2 * page + 1 : 2 * page + 2]
            visible.append((row_of == owner) & (lane < filled))
            blocks.append(scores[:, page * PAGE : (page + 1) * PAGE])
    top = jnp.full(shape, NEG_BIG, jnp.float32)
    for seen, block in zip(visible, blocks):
        top = jnp.maximum(top, jnp.where(seen, block, NEG_BIG))
    chip_max = jnp.max(top, axis=1, keepdims=True)
    weights = [
        jnp.where(seen, jnp.exp(block - chip_max), 0.0) for seen, block in zip(visible, blocks)
    ]
    total = jnp.sum(functools.reduce(jnp.add, weights), axis=1, keepdims=True)
    latent = jnp.zeros((query.shape[0], LAT), jnp.float32)
    pages = own.shape[1] // PAGE
    for side, cache in enumerate((own, other)):
        low = jnp.concatenate(weights[side * pages : (side + 1) * pages], axis=1)
        latent += lax.dot_general(
            low.astype(jnp.bfloat16),
            cache[:LAT, :],
            (((1,), (1,)), ((), ())),
            preferred_element_type=jnp.float32,
        )
    lines = rows * heads
    stats = stats_tile(chip_max, total).T[:STATS].astype(jnp.bfloat16)
    latent = latent.astype(jnp.bfloat16)
    chip = lax.div(lax.axis_index("ctx"), 2)
    for at, mask in enumerate(masks):
        target = at if before is None else chip ^ mask
        for tile in range(LAT // LANES):
            columns = slice(tile * LANES, (tile + 1) * LANES)
            block = latent[at * lines : (at + 1) * lines, columns]
            message[target, tile * lines : (tile + 1) * lines] = block
        message[target, LAT // LANES * lines :] = stats
    if before is not None:
        finished, finished_masks = before
        for at, mask in enumerate(finished_masks):
            message[chip ^ mask] = finished[at]


def near_kernel(rows, heads, masks, *refs):
    tables, queries, (own, other, message) = refs[:2], refs[2:-3], refs[-3:]
    attend_kernel(rows, heads, masks, tables, queries, own, other, None, message)


def far_kernel(rows, heads, masks, near_masks, *refs):
    tables, queries, (own, other, near, message) = refs[:2], refs[2:-4], refs[-4:]
    before = (near, near_masks)
    attend_kernel(rows, heads, masks, tables, queries, own, other, before, message)


def own_span(width_dev):
    index = lax.axis_index("ctx")
    span = math.lcm(width_dev, LANES)
    start = pl.multiple_of(lax.div(index, span // width_dev) * span, LANES)
    return (start, span, lax.rem(index, span // width_dev))


def project(flat, out_proj, start, target):
    step = math.gcd(target.shape[1], COLUMN_BLOCK)
    for at in range(0, target.shape[1], step):
        columns = pl.ds(pl.multiple_of(start + at, LANES), step)
        terms = jnp.dot(flat, out_proj[:, columns], preferred_element_type=jnp.float32)
        target[:, at : at + step] = terms


def add_residual(hidden, wanted, target):
    rows, width_dev = hidden.shape
    half = target.shape[1]
    start, span, place = own_span(width_dev)

    @pl.when(lax.div(start, half) == wanted)
    def _():
        own = hidden[...].astype(jnp.float32)
        residual = jnp.zeros((rows, span), jnp.float32)
        for at in range(span // width_dev):
            before, after = at * width_dev, span - (at + 1) * width_dev
            pieces = [jnp.zeros((rows, before), jnp.float32)] * (before > 0) + [own]
            pieces += [jnp.zeros((rows, after), jnp.float32)] * (after > 0)
            residual = jnp.where(place == at, jnp.concatenate(pieces, axis=1), residual)
        target[:, pl.ds(pl.multiple_of(lax.rem(start, half), LANES), span)] += residual


def heads_kernel(
    rows, heads, orders, parts, absorb, out_proj, hidden, send, flat_out, latent_buf, stats_buf
):
    lines = rows * heads
    tiles = range(LAT // LANES)
    last = LAT // LANES * lines
    own_chip = lax.div(lax.axis_index("ctx"), 2)
    masks = [mask for order in orders for mask in order]
    places = [place for order in orders for place in range(len(order))]
    gathered = [parts[own_chip ^ mask, last:].astype(jnp.float32) for mask in masks]
    stats_buf[...] = jnp.concatenate(gathered, axis=0).T
    stats = []
    for at, place in enumerate(places):
        block = stats_buf[place * lines : (place + 1) * lines, :]
        stats.append(from_stats(block[:, at * STATS : (at + 1) * STATS]))
    joint = functools.reduce(jnp.maximum, [shard_max for shard_max, _ in stats])
    factors = [jnp.exp(shard_max - joint) for shard_max, _ in stats]
    total = sum(part_total * factor for (_, part_total), factor in zip(stats, factors))
    for tile in tiles:
        latent = jnp.zeros((lines, LANES), jnp.float32)
        for mask, factor in zip(masks, factors):
            part = parts[own_chip ^ mask, tile * lines : (tile + 1) * lines]
            latent += part.astype(jnp.float32) * factor
        latent_buf[tile] = latent / total
    value_heads = []
    for head in range(heads):
        picked = pl.ds(head, rows, stride=heads)
        own = jnp.concatenate([latent_buf[tile, picked, :] for tile in tiles], axis=1)
        own = own.astype(jnp.bfloat16)
        value_heads.append(jnp.dot(own, absorb[head], preferred_element_type=jnp.float32))
    flat = jnp.concatenate(value_heads, axis=1).astype(jnp.bfloat16)
    flat_out[...] = flat
    other_core = 1 - lax.rem(lax.axis_index("ctx"), 2)
    project(flat, out_proj, other_core * send.shape[1], send)
    add_residual(hidden, other_core, send)


def keep_kernel(flat, out_proj, hidden, keep):
    core = lax.rem(lax.axis_index("ctx"), 2)
    project(flat[...], out_proj, core * keep.shape[1], keep)
    add_residual(hidden, core, keep)


def expand(side, start, gain, gate, up):
    rows, half = side.shape
    units = gate.shape[0]
    step = math.gcd(half, COLUMN_BLOCK)
    both = jnp.zeros((rows, 2 * units), jnp.float32)
    for at in range(0, half, step):
        columns = pl.ds(pl.multiple_of(start + at, LANES), step)
        scaled = (side[:, at : at + step] * gain[:, columns]).astype(jnp.bfloat16)
        both += lax.dot_general(
            scaled,
            jnp.concatenate([gate[:, columns], up[:, columns]], axis=0),
            (((1,), (1,)), ((), ())),
            preferred_element_type=jnp.float32,
        )
    return both


def own_half_kernel(mine, gain, gate, up, both):
    core = lax.rem(lax.axis_index("ctx"), 2)
    both[...] = expand(mine, core * mine.shape[1], gain, gate, up)


def ffn_kernel(mine, other, both, gain, gate, up, down, blocks, stream_own):
    _, half = mine.shape
    width, units = 2 * half, gate.shape[0]
    core = lax.rem(lax.axis_index("ctx"), 2)
    square = jnp.sum(mine[...] * mine[...], axis=1, keepdims=True)
    square += jnp.sum(other[...] * other[...], axis=1, keepdims=True)
    norm_scale = lax.rsqrt(square / width + EPS)
    acts = (both[...] + expand(other, (1 - core) * half, gain, gate, up)) * norm_scale
    gate_act, up_act = acts[:, :units], acts[:, units:]
    activated = (gate_act / (1.0 + jnp.exp(-gate_act)) * up_act).astype(jnp.bfloat16)
    _, _, width_dev = blocks.shape
    step = math.lcm(width_dev, LANES)
    for at in range(0, width, step):
        terms = jnp.dot(activated, down[:, at : at + step], preferred_element_type=jnp.float32)
        terms = terms.astype(jnp.bfloat16)
        for inner in range(0, step, width_dev):
            blocks[(at + inner) // width_dev] = terms[:, inner : inner + width_dev]
    start, span, place = own_span(width_dev)
    in_half = pl.ds(pl.multiple_of(lax.rem(start, half), LANES), span)
    near = jnp.where(lax.div(start, half) == core, mine[:, in_half], other[:, in_half])
    own = near[:, :width_dev]
    for at in range(1, span // width_dev):
        own = jnp.where(place == at, near[:, at * width_dev : (at + 1) * width_dev], own)
    stream_own[...] = own


def shards(
    queries,
    cache,
    page_row,
    page_index,
    lengths,
    hidden_in,
    norm_gain,
    absorb_value,
    out_proj,
    gate_proj,
    up_proj,
    down_proj,
):
    rows, heads, entry = queries.shape
    count = lax.axis_size("ctx")
    chips = count // 2
    width_dev = hidden_in.shape[1]
    width = out_proj.shape[1]
    half = width // 2
    lines = rows * heads
    bf16, f32 = jnp.bfloat16, jnp.float32
    shaped = jax.ShapeDtypeStruct

    mark = call(first_kernel, shaped((8, LANES), f32), [], (), ahead=(cache, cache), scale=0.1)
    blocks, mark = gather_blocks(queries.reshape(lines, entry), mark)
    cache_sent, mark = lax.optimization_barrier((cache, mark))
    cache_t = cache.T
    cache_other = swap(cache_sent.T)
    pages = page_row.shape[0]
    table = call(
        table_kernel,
        shaped((2 * pages, LANES), jnp.int32),
        [VMEM] * 4,
        (page_row[None], page_index[None], lengths[None], mark),
    )
    tables = (table, swap(table))
    near_masks = [mask for mask in blocks if mask % 2 == 0]
    far_masks = [mask for mask in blocks if mask % 2 == 1]
    block_shape = (LAT // LANES * lines + STATS, LANES)
    near = call(
        functools.partial(near_kernel, rows, heads, near_masks),
        shaped((len(near_masks),) + block_shape, bf16),
        [VMEM] * (len(near_masks) + 4),
        tables + tuple(blocks[mask] for mask in near_masks) + (cache_t, cache_other),
    )
    message = call(
        functools.partial(far_kernel, rows, heads, far_masks, near_masks),
        shaped((chips,) + block_shape, bf16),
        [VMEM] * (len(far_masks) + 5),
        tables + tuple(blocks[mask] for mask in far_masks) + (cache_t, cache_other, near),
        ahead=(absorb_value, out_proj),
    )
    parts = exchange(message)
    send, flat = call(
        functools.partial(heads_kernel, rows, heads, (near_masks, far_masks)),
        (shaped((rows, half), f32), shaped((rows, absorb_value.shape[0] * VHEAD), bf16)),
        [VMEM] * 4,
        (parts, absorb_value, out_proj, hidden_in),
        scratch=[
            pltpu.VMEM((LAT // LANES, lines, LANES), f32),
            pltpu.VMEM((LANES, chips * STATS), f32),
        ],
        ahead=(gate_proj, up_proj, down_proj),
    )
    keep = call(
        keep_kernel, shaped((rows, half), f32), [VMEM] * 3, (flat, out_proj, hidden_in)
    )
    chip_terms = (keep + swap(send)).astype(bf16)
    mine = jnp.sum(spread(chip_terms).astype(f32), axis=0)
    other = swap(mine)
    weights = (norm_gain[None], gate_proj.T, up_proj.T)
    both = call(
        own_half_kernel,
        shaped((rows, 2 * gate_proj.shape[1]), f32),
        [VMEM] * 4,
        (mine,) + weights,
    )
    blocks, stream_own = call(
        ffn_kernel,
        (shaped((count, rows, width_dev), bf16), shaped((rows, width_dev), f32)),
        [VMEM] * 7,
        (mine, other, both) + weights + (down_proj,),
    )
    received = lax.all_to_all(blocks, "ctx", 0, 0, tiled=True)
    return (stream_own + jnp.sum(received.astype(f32), axis=0)).astype(bf16)


def solution(mesh):
    in_specs = (
        P("groups", "ctx", None),
        P(("groups", "ctx"), None),
        P(("groups", "ctx")),
        P(("groups", "ctx")),
        P("groups"),
        P("groups", "ctx"),
        P(),
        P("ctx", None, None),
        P("ctx", None),
        P(None, "ctx"),
        P(None, "ctx"),
        P("ctx", None),
    )
    out_specs = P("groups", "ctx")
    return jax.shard_map(shards, mesh=mesh, in_specs=in_specs, out_specs=out_specs, check_vma=False)
```
